512 devices in a mesh: tm: 16 (over y, x_hi), gz: 32 (over x_lo, z, core).
Axes of the slice: x: 4 (x_hi: 2, x_lo: 2; x = x_hi * 2 + x_lo), y: 8, z: 8, core: 2. Of those that a mesh axis runs over, the one named last changes fastest.
Arguments:
- states: float32 [16, 4, 128, 64, 128], P('tm', None, 'gz'), may hold values from -6 to 6
- shift: int32 [1], replicated, may hold values from 0 to 127
- step_size: float32 [1], replicated, may hold values from 0.1 to 0.5
Outputs:
- updated: float32 [16, 4, 128, 64, 128], P('tm', None, 'gz')
- mismatch: float32 [16, 4, 128, 64, 128], P('tm', None, 'gz')
The draws below stay inside these ranges and needn't reach their ends.
All inputs are finite; a program needn't handle non-finite values.
Results may differ from the reference program's by a relative error of at most 0.00002.
Values sent between devices are 32-bit elements; how exact they have to be, the bound alone decides.
No kernel may reach another device: no remote copies, remote signals or barrier semaphores. Data moves between devices by JAX's collectives and lax.ppermute only.
A program may use at most 64 MiB of HBM per device.

```python
import math
import jax
import jax.numpy as jnp
from jax import lax

R = 64
TH = 128
STEPS = 1
SWEEPS = 3
SECTIONS = 16
NZ = 128


def level_of(stream_key, extent, cuts, least, high):
    loudness = 1.0
    for axis_at, blocks in cuts:
        draws = jax.random.uniform(jax.random.fold_in(jax.random.fold_in(stream_key, 6), axis_at), (blocks,), jnp.float32, least / len(cuts), high / len(cuts))
        loudness = loudness * jnp.repeat(jnp.exp(draws), extent[axis_at] // blocks).reshape((-1,) + (1,) * (len(extent) - 1 - axis_at))
    return loudness


def gaussian(key, extent, deviation, limit, cuts=(), kind=jnp.bfloat16):
    values = deviation * jax.random.normal(key, extent, jnp.float32)
    if cuts:
        values = values * level_of(key, extent, cuts, -0.22, 0.18)
    return jnp.clip(values, -limit, limit).astype(kind)


def setup_inputs(seed: int = 0) -> dict:
    arg_keys = jax.random.split(jax.random.key(seed), 4)
    return {
        "states": gaussian(arg_keys[0], (SECTIONS, 4, NZ, R, TH), 1.0, 6.0, ((0, 16), (2, 32)), jnp.float32),
        "shift": jax.random.randint(arg_keys[1], (1,), 0, TH).astype(jnp.int32),
        "step_size": jnp.clip(jnp.exp(jax.random.uniform(arg_keys[2], (1,), jnp.float32, math.log(0.1), math.log(0.5))), 0.1, 0.5),
    }


time_step = 0.2
viscous = 1.0

def base_speed(rows):
    radius = 1.0 + (jnp.arange(rows, dtype=jnp.float32) + 0.5) / rows
    return (0.2 + 0.6 / (radius * radius))[:, None]

def radial_pad(centre):
    return jnp.pad(centre, ((0, 0), (0, 0), (1, 1), (0, 0)))

def explicit(padded, flow_speed):
    centre = padded[:, 1:-1]
    along_z = (padded[:, 2:] - padded[:, :-2]) * 0.5
    along_th = (jnp.roll(centre, -1, 3) - jnp.roll(centre, 1, 3)) * 0.5
    walled = radial_pad(centre)
    along_r = (walled[:, :, 2:] - walled[:, :, :-2]) * 0.5
    radial, azimuth, axial, pressure = (centre[0], centre[1], centre[2], centre[3])
    advect = (flow_speed + azimuth) * along_th + radial * along_r + axial * along_z
    new_radial = radial - time_step * (advect[0] - 2.0 * flow_speed * azimuth + along_r[3])
    new_azimuth = azimuth - time_step * (advect[1] + flow_speed * radial + along_th[3])
    new_axial = axial - time_step * (advect[2] + along_z[3])
    new_pressure = pressure - time_step * (along_r[0] + along_th[1] + along_z[2])
    return jnp.stack([new_radial, new_azimuth, new_axial, new_pressure])

def inner_sum(padded):
    centre = padded[:, 1:-1]
    walled = radial_pad(centre)
    total = padded[:, 2:] + padded[:, :-2]
    total = total + jnp.roll(centre, 1, 3) + jnp.roll(centre, -1, 3)
    return total + walled[:, :, 2:] + walled[:, :, :-2]

def wrap_axial(field):
    return jnp.concatenate([field[:, -1:], field, field[:, :1]], axis=1)

def one_step(field, flow_speed):
    force = explicit(wrap_axial(field), flow_speed)
    iterate = force
    for number in range(SWEEPS):
        iterate = (force + viscous * inner_sum(wrap_axial(iterate))) / (1.0 + 6.0 * viscous)
    return iterate

def section(field, flow_speed):
    stepper = jax.checkpoint(one_step)
    for number in range(STEPS):
        field = stepper(field, flow_speed)
    return field

def reference(states, shift, step_size):
    flow_speed = base_speed(R)
    offset = shift[0]
    ends = lax.map(lambda field: section(field, flow_speed), states)
    following = jnp.concatenate([states[1:], jnp.roll(states[:1], offset, axis=4)], axis=0)
    mismatch = ends - following

    def pull_back(pair):
        start, cotangent = pair
        _, puller = jax.vjp(lambda field: section(field, flow_speed), start)
        return puller(cotangent)[0]
    adjoint = lax.map(pull_back, (states, mismatch))
    prior = jnp.concatenate([jnp.roll(mismatch[-1:], -offset, axis=4), mismatch[:-1]], axis=0)
    updated = states - step_size[0] * (adjoint - prior)
    return (updated, mismatch)
```

```python
import jax
import jax.numpy as jnp
from jax import lax
from jax.experimental import pallas as pl
from jax.experimental.pallas import tpu as pltpu
from jax.sharding import PartitionSpec as P

SWEEPS = 3
TAU = 0.2
HALF_TAU = 0.5 * TAU
VISCOUS = 1.0
SCALE = 1.0 / (1.0 + 6.0 * VISCOUS)


def base_speed(shape):
    rows = shape[0]
    cell = lax.broadcasted_iota(jnp.int32, shape, 0).astype(jnp.float32)
    radius = 1.0 + (cell + 0.5) / rows
    return 0.2 + 0.6 / (radius * radius)


def lane_up(f):
    return pltpu.roll(f, f.shape[1] - 1, 1)


def lane_down(f):
    return pltpu.roll(f, 1, 1)


class Walls:
    def __init__(self, shape):
        row = lax.broadcasted_iota(jnp.int32, shape, 0)
        self.first = row == 0
        self.last = row == shape[0] - 1
        self.rows = shape[0]

    def up(self, f):
        return jnp.where(self.last, 0.0, pltpu.roll(f, self.rows - 1, 0))

    def down(self, f):
        return jnp.where(self.first, 0.0, pltpu.roll(f, 1, 0))


def place(layer, depth, odd):
    k = layer % depth
    return k + odd * (depth - 1 - 2 * k)


def layer_of(refs, field, layer, depth, odd):
    behind, own, ahead = refs
    ref = behind if layer < 0 else own if layer < depth else ahead
    return ref[field, place(layer, depth, odd)]


def in_plane(f, walls):
    return lane_up(f) + lane_down(f) + walls.up(f) + walls.down(f)


def forward_kernel(own, chip, cross, ends, force, first, second):
    fields, depth, rows, columns = own.shape
    odd = lax.axis_index("gz") % 2
    sign = (1 - 2 * odd).astype(jnp.float32)
    walls = Walls((rows, columns))
    speed = base_speed((rows, columns))
    refs = (cross, own, chip)

    def at(field, layer):
        return layer_of(refs, field, layer, depth, odd)

    reach = SWEEPS
    for layer in range(-reach, depth + reach):
        here = [at(f, layer) for f in range(fields)]
        d_z = [at(f, layer + 1) - at(f, layer - 1) for f in range(fields)]
        d_th = [lane_up(f) - lane_down(f) for f in here]
        d_r = [walls.up(f) - walls.down(f) for f in here]
        u, v, w, p = here
        by_th = HALF_TAU * (speed + v)
        by_r = HALF_TAU * u
        by_z = (HALF_TAU * sign) * w
        to = layer + reach
        carried = [by_th * d_th[f] + by_r * d_r[f] + by_z * d_z[f] for f in range(3)]
        force[0, to] = u - (carried[0] + HALF_TAU * d_r[3]) + (2.0 * TAU) * speed * v
        force[1, to] = v - (carried[1] + HALF_TAU * d_th[3]) - TAU * speed * u
        force[2, to] = w - (carried[2] + (HALF_TAU * sign) * d_z[3])
        force[3, to] = p - HALF_TAU * (d_r[0] + d_th[1] + sign * d_z[2])

    def sweep(source, source_reach, put):
        reach = source_reach - 1
        for layer in range(-reach, depth + reach):
            for f in range(fields):
                k = layer + source_reach
                total = force[f, layer + SWEEPS] + source[f, k - 1] + source[f, k + 1]
                total = total + in_plane(source[f, k], walls)
                put(f, layer, total * SCALE)

    def put_first(f, layer, value):
        first[f, layer + 2] = value

    def put_second(f, layer, value):
        second[f, layer + 1] = value

    def put_ends(f, layer, value):
        ends[f, place(layer, depth, odd)] = value

    sweep(force, 3, put_first)
    sweep(first, 2, put_second)
    sweep(second, 1, put_ends)


def turn(field, amount):
    return pltpu.roll(field, amount, 1)


def mismatch_kernel(shift, ends, following, mismatch):
    fields, depth, rows, columns = ends.shape
    last = lax.axis_index("tm") == lax.axis_size("tm") - 1
    amount = jnp.where(last, shift[0], 0)
    for f in range(fields):
        for k in range(depth):
            mismatch[f, k] = ends[f, k] - turn(following[f, k], amount)


def adjoint_kernel(
    shift, step_size, own, chip, cross, own_mis, chip_mis, cross_mis, prior_ends, updated, cot, first, second
):
    fields, depth, rows, columns = own.shape
    odd = lax.axis_index("gz") % 2
    sign = (1 - 2 * odd).astype(jnp.float32)
    walls = Walls((rows, columns))
    speed = base_speed((rows, columns))
    refs = (cross, own, chip)
    mis = (cross_mis, own_mis, chip_mis)

    def at(field, layer):
        return layer_of(refs, field, layer, depth, odd)

    def mis_at(field, layer):
        return layer_of(mis, field, layer, depth, odd)

    for f in range(fields):
        for layer in range(-3, depth + 3):
            here = mis_at(f, layer)
            total = mis_at(f, layer - 1) + mis_at(f, layer + 1) + in_plane(here, walls)
            total = total * SCALE
            first[f, layer + 3] = total
            if -1 <= layer <= depth:
                cot[f, layer + 1] = (here + total) * SCALE
        for layer in range(-2, depth + 2):
            k = layer + 3
            total = first[f, k - 1] + first[f, k + 1] + in_plane(first[f, k], walls)
            total = total * SCALE
            second[f, layer + 2] = total
            if -1 <= layer <= depth:
                cot[f, layer + 1] = cot[f, layer + 1] + total * SCALE
        for layer in range(-1, depth + 1):
            k = layer + 2
            total = second[f, k - 1] + second[f, k + 1] + in_plane(second[f, k], walls)
            cot[f, layer + 1] = cot[f, layer + 1] + total * SCALE

    is_first = lax.axis_index("tm") == 0
    amount = jnp.where(is_first, columns - shift[0], 0) % columns
    size = step_size[0]
    half = HALF_TAU
    for layer in range(depth):
        k = layer + 1
        here = [at(f, layer) for f in range(fields)]
        u, v, w, p = here
        c = [cot[f, k] for f in range(fields)]
        below = [cot[f, k - 1] for f in range(fields)]
        above = [cot[f, k + 1] for f in range(fields)]
        w_below, w_above = at(2, layer - 1), at(2, layer + 1)
        d_z = [at(f, layer + 1) - at(f, layer - 1) for f in range(3)]
        d_th = [lane_up(f) - lane_down(f) for f in here[:3]]
        d_r = [walls.up(f) - walls.down(f) for f in here[:3]]
        swirl = speed + v

        def th(f):
            return lane_up(f) - lane_down(f)

        def rad(f):
            return walls.up(f) - walls.down(f)

        pull_r = c[0] * d_r[0] + c[1] * d_r[1] + c[2] * d_r[2]
        pull_th = c[0] * d_th[0] + c[1] * d_th[1] + c[2] * d_th[2]
        pull_z = c[0] * d_z[0] + c[1] * d_z[1] + c[2] * d_z[2]
        axial = [w_above * above[f] - w_below * below[f] for f in range(3)]
        grads = [
            c[0]
            + half * (th(swirl * c[0]) + rad(u * c[0] + c[3]) + sign * axial[0] - pull_r)
            - TAU * speed * c[1],
            c[1]
            + half * (th(swirl * c[1] + c[3]) + rad(u * c[1]) + sign * axial[1] - pull_th)
            + (2.0 * TAU) * speed * c[0],
            c[2]
            + half
            * (
                th(swirl * c[2])
                + rad(u * c[2])
                + sign * (axial[2] + above[3] - below[3] - pull_z)
            ),
            c[3] + half * (rad(c[0]) + th(c[1]) + sign * (above[2] - below[2])),
        ]
        to = place(layer, depth, odd)
        for f in range(fields):
            prior = turn(prior_ends[f, to], amount) - here[f]
            updated[f, to] = here[f] - size * (grads[f] - prior)


VMEM = pl.BlockSpec(memory_space=pltpu.VMEM)
PARAMS = pltpu.CompilerParams(vmem_limit_bytes=16 * 2**20)
SMEM = pl.BlockSpec(memory_space=pltpu.SMEM)


def scratch(shape, layers):
    return pltpu.VMEM((shape[0], layers) + shape[2:], jnp.float32)


def cost(shape, passes):
    size = shape[0] * shape[1] * shape[2] * shape[3]
    return pl.CostEstimate(flops=passes * size, bytes_accessed=4 * size, transcendentals=0)


def forward(own, chip, cross):
    shape = own.shape
    depth = shape[1]
    return pl.pallas_call(
        forward_kernel,
        out_shape=jax.ShapeDtypeStruct(shape, jnp.float32),
        in_specs=[VMEM] * 3,
        out_specs=VMEM,
        scratch_shapes=[scratch(shape, depth + 6), scratch(shape, depth + 4), scratch(shape, depth + 2)],
        cost_estimate=cost(shape, 100),
        compiler_params=PARAMS,
        name="forward",
    )(own, chip, cross)


def compare(shift, ends, following):
    return pl.pallas_call(
        mismatch_kernel,
        out_shape=jax.ShapeDtypeStruct(ends.shape, jnp.float32),
        in_specs=[SMEM, VMEM, VMEM],
        out_specs=VMEM,
        cost_estimate=cost(ends.shape, 2),
        compiler_params=PARAMS,
        name="compare",
    )(shift, ends, following)


def adjoint(shift, step_size, slabs, mismatches, prior_ends):
    shape = prior_ends.shape
    depth = shape[1]
    return pl.pallas_call(
        adjoint_kernel,
        out_shape=jax.ShapeDtypeStruct(shape, jnp.float32),
        in_specs=[SMEM, SMEM] + [VMEM] * 7,
        out_specs=VMEM,
        scratch_shapes=[scratch(shape, depth + 2), scratch(shape, depth + 6), scratch(shape, depth + 4)],
        cost_estimate=cost(shape, 150),
        compiler_params=PARAMS,
        name="adjoint",
    )(shift, step_size, *slabs, *mismatches, prior_ends)


def per_device(states, shift, step_size):
    start = states[0]
    slabs, sections = lax.axis_size("gz"), lax.axis_size("tm")
    same_chip = [(i, i ^ 1) for i in range(slabs)]
    next_chip = [(i, (i + 1 if i % 2 else i - 1) % slabs) for i in range(slabs)]
    forth = [(i, (i + 1) % sections) for i in range(sections)]
    back = [((i + 1) % sections, i) for i in range(sections)]

    cross = lax.ppermute(start, "gz", next_chip)
    chip = lax.ppermute(start, "gz", same_chip)
    following = lax.ppermute(start, "tm", back)
    ends = forward(start, chip, cross)
    prior_ends = lax.ppermute(ends, "tm", forth)
    mismatch = compare(shift, ends, following)
    cross_mis = lax.ppermute(mismatch, "gz", next_chip)
    chip_mis = lax.ppermute(mismatch, "gz", same_chip)
    updated = adjoint(shift, step_size, (start, chip, cross), (mismatch, chip_mis, cross_mis), prior_ends)
    return updated[None], mismatch[None]


def solution(mesh):
    placed = P("tm", None, "gz", None, None)
    return jax.shard_map(
        per_device,
        mesh=mesh,
        in_specs=(placed, P(), P()),
        out_specs=(placed, placed),
        check_vma=False,
    )
```

```python
import jax
import jax.numpy as jnp
from jax import lax
from jax.experimental import pallas as pl
from jax.experimental.pallas import tpu as pltpu
from jax.sharding import PartitionSpec as P

SWEEPS = 3
TAU = 0.2
HALF_TAU = 0.5 * TAU
VISCOUS = 1.0
SCALE = 1.0 / (1.0 + 6.0 * VISCOUS)


def base_speed(shape):
    rows = shape[0]
    cell = lax.broadcasted_iota(jnp.int32, shape, 0).astype(jnp.float32)
    radius = 1.0 + (cell + 0.5) / rows
    return 0.2 + 0.6 / (radius * radius)


def lane_up(f):
    return pltpu.roll(f, f.shape[1] - 1, 1)


def lane_down(f):
    return pltpu.roll(f, 1, 1)


class Walls:
    def __init__(self, shape):
        row = lax.broadcasted_iota(jnp.int32, shape, 0)
        self.first = row == 0
        self.last = row == shape[0] - 1
        self.rows = shape[0]

    def up(self, f):
        return jnp.where(self.last, 0.0, pltpu.roll(f, self.rows - 1, 0))

    def down(self, f):
        return jnp.where(self.first, 0.0, pltpu.roll(f, 1, 0))


def place(layer, depth, odd):
    k = layer % depth
    return k + odd * (depth - 1 - 2 * k)


def layer_of(refs, field, layer, depth, odd):
    behind, own, ahead = refs
    ref = behind if layer < 0 else own if layer < depth else ahead
    return ref[field, place(layer, depth, odd)]


def in_plane(f, walls):
    return lane_up(f) + lane_down(f) + walls.up(f) + walls.down(f)


def explicit(at, put, layers, sign, walls, speed):
    for layer in layers:
        here = [at(f, layer) for f in range(4)]
        d_z = [at(f, layer + 1) - at(f, layer - 1) for f in range(4)]
        d_th = [lane_up(f) - lane_down(f) for f in here]
        d_r = [walls.up(f) - walls.down(f) for f in here]
        u, v, w, p = here
        by_th = HALF_TAU * (speed + v)
        by_r = HALF_TAU * u
        by_z = (HALF_TAU * sign) * w
        carried = [by_th * d_th[f] + by_r * d_r[f] + by_z * d_z[f] for f in range(3)]
        put(0, layer, u - (carried[0] + HALF_TAU * d_r[3]) + (2.0 * TAU) * speed * v)
        put(1, layer, v - (carried[1] + HALF_TAU * d_th[3]) - TAU * speed * u)
        put(2, layer, w - (carried[2] + (HALF_TAU * sign) * d_z[3]))
        put(3, layer, p - HALF_TAU * (d_r[0] + d_th[1] + sign * d_z[2]))


def neighbours(at, field, layer, walls):
    return at(field, layer - 1) + at(field, layer + 1) + in_plane(at(field, layer), walls)


class Level:
    def __init__(self, *parts):
        self.parts = parts

    def find(self, layer):
        for ref, low, high, start in self.parts:
            if low <= layer < high:
                return ref, start + layer - low

    def get(self, field, layer):
        ref, k = self.find(layer)
        return ref[field, k]

    def put(self, field, layer, value):
        for ref, low, high, start in self.parts:
            if low <= layer < high:
                ref[field, start + layer - low] = value


def facing(own):
    depth = own.shape[1]
    odd = lax.axis_index("gz") % 2
    return depth, odd, (1 - 2 * odd).astype(jnp.float32), Walls(own.shape[2:]), base_speed(own.shape[2:])


def forward_cross_kernel(own, cross, partial, force, first):
    depth, odd, sign, walls, speed = facing(own)

    def at(field, layer):
        return layer_of((cross, own, None), field, layer, depth, odd)

    e = Level((force, -3, 0, 0), (partial, 0, depth - 1, 0))
    one = Level((first, -2, 0, 0), (partial, 0, 2, 3))
    two = Level((partial, -1, 1, 5))
    explicit(at, e.put, range(-3, depth - 1), sign, walls, speed)
    for f in range(4):
        for layer in range(-2, 2):
            one.put(f, layer, (e.get(f, layer) + neighbours(e.get, f, layer, walls)) * SCALE)
        for layer in range(-1, 1):
            two.put(f, layer, (e.get(f, layer) + neighbours(one.get, f, layer, walls)) * SCALE)


def forward_chip_kernel(own, chip, partial, ends, force, first, second):
    depth, odd, sign, walls, speed = facing(own)

    def at(field, layer):
        return layer_of((None, own, chip), field, layer, depth, odd)

    e = Level((partial, 0, depth - 1, 0), (force, depth - 1, depth + 3, 0))
    one = Level((partial, 0, 2, 3), (first, 2, depth + 2, 0))
    two = Level((partial, -1, 1, 5), (second, 1, depth + 1, 0))
    explicit(at, e.put, range(depth - 1, depth + 3), sign, walls, speed)
    for f in range(4):
        for layer in range(2, depth + 2):
            one.put(f, layer, (e.get(f, layer) + neighbours(e.get, f, layer, walls)) * SCALE)
        for layer in range(1, depth + 1):
            two.put(f, layer, (e.get(f, layer) + neighbours(one.get, f, layer, walls)) * SCALE)
        for layer in range(depth):
            total = e.get(f, layer) + neighbours(two.get, f, layer, walls)
            ends[f, place(layer, depth, odd)] = total * SCALE


def turn(field, amount):
    return pltpu.roll(field, amount, 1)


def compare_kernel(shift, ends, following, mismatch):
    fields, depth, rows, columns = ends.shape
    last = lax.axis_index("tm") == lax.axis_size("tm") - 1
    amount = jnp.where(last, shift[0], 0)
    for f in range(fields):
        for k in range(depth):
            mismatch[f, k] = ends[f, k] - turn(following[f, k], amount)


def carry_kernel(shift, own, prior_ends, prior):
    fields, depth, rows, columns = own.shape
    is_first = lax.axis_index("tm") == 0
    amount = jnp.where(is_first, columns - shift[0], 0) % columns
    for f in range(fields):
        for k in range(depth):
            prior[f, k] = turn(prior_ends[f, k], amount) - own[f, k]


def adjoint_cross_kernel(own_mis, cross_mis, partial, first, second):
    depth, odd, sign, walls, speed = facing(own_mis)

    def c(field, layer):
        return layer_of((cross_mis, own_mis, None), field, layer, depth, odd)

    one = Level((first, -3, 1, 0), (partial, 1, 3, 2))
    two = Level((second, -2, 0, 0), (partial, 0, 2, 4))
    for f in range(4):
        for layer in range(-3, 3):
            one.put(f, layer, neighbours(c, f, layer, walls) * SCALE)
        for layer in range(-2, 2):
            two.put(f, layer, neighbours(one.get, f, layer, walls) * SCALE)
        for layer in range(-1, 1):
            last = neighbours(two.get, f, layer, walls)
            partial[f, layer + 1] = (c(f, layer) + one.get(f, layer) + two.get(f, layer) + last) * SCALE


def adjoint_chip_kernel(step_size, own, chip, cross, own_mis, chip_mis, prior, partial, updated, cot, first, second):
    depth, odd, sign, walls, speed = facing(own)

    def at(field, layer):
        return layer_of((cross, own, chip), field, layer, depth, odd)

    def c(field, layer):
        return layer_of((None, own_mis, chip_mis), field, layer, depth, odd)

    one = Level((partial, 1, 3, 2), (first, 3, depth + 3, 0))
    two = Level((partial, 0, 2, 4), (second, 2, depth + 2, 0))
    total = Level((partial, -1, 1, 0), (cot, 1, depth + 1, 0))
    for f in range(4):
        for layer in range(3, depth + 3):
            one.put(f, layer, neighbours(c, f, layer, walls) * SCALE)
        for layer in range(2, depth + 2):
            two.put(f, layer, neighbours(one.get, f, layer, walls) * SCALE)
        for layer in range(1, depth + 1):
            last = neighbours(two.get, f, layer, walls)
            total.put(f, layer, (c(f, layer) + one.get(f, layer) + two.get(f, layer) + last) * SCALE)

    size = step_size[0]
    half = HALF_TAU

    def th(f):
        return lane_up(f) - lane_down(f)

    def rad(f):
        return walls.up(f) - walls.down(f)

    for layer in range(depth):
        here = [at(f, layer) for f in range(4)]
        u, v, w, p = here
        c0, c1, c2, c3 = (total.get(f, layer) for f in range(4))
        below = [total.get(f, layer - 1) for f in range(4)]
        above = [total.get(f, layer + 1) for f in range(4)]
        w_below, w_above = at(2, layer - 1), at(2, layer + 1)
        swirl = speed + v
        pull_r = c0 * rad(u) + c1 * rad(v) + c2 * rad(w)
        pull_th = c0 * th(u) + c1 * th(v) + c2 * th(w)
        pull_z = sum(x * (at(f, layer + 1) - at(f, layer - 1)) for f, x in ((0, c0), (1, c1), (2, c2)))
        axial = [w_above * above[f] - w_below * below[f] for f in range(3)]
        grads = [
            c0 + half * (th(swirl * c0) + rad(u * c0 + c3) + sign * axial[0] - pull_r) - TAU * speed * c1,
            c1
            + half * (th(swirl * c1 + c3) + rad(u * c1) + sign * axial[1] - pull_th)
            + (2.0 * TAU) * speed * c0,
            c2 + half * (th(swirl * c2) + rad(u * c2) + sign * (axial[2] + above[3] - below[3] - pull_z)),
            c3 + half * (rad(c0) + th(c1) + sign * (above[2] - below[2])),
        ]
        to = place(layer, depth, odd)
        for f in range(4):
            updated[f, to] = here[f] - size * (grads[f] - prior[f, to])


def copy_kernel(source, own):
    for f in range(source.shape[0]):
        for k in range(source.shape[1]):
            own[f, k] = source[f, k]


VMEM = pl.BlockSpec(memory_space=pltpu.VMEM)
PARAMS = pltpu.CompilerParams(vmem_limit_bytes=16 * 2**20)
SMEM = pl.BlockSpec(memory_space=pltpu.SMEM)


def kernel(body, like, ins, out_layers, scratch_layers=(), name=None, passes=50):
    fields, depth, rows, columns = like.shape
    size = fields * depth * rows * columns
    return pl.pallas_call(
        body,
        out_shape=jax.ShapeDtypeStruct((fields, out_layers, rows, columns), jnp.float32),
        in_specs=ins,
        out_specs=VMEM,
        scratch_shapes=[pltpu.VMEM((fields, n, rows, columns), jnp.float32) for n in scratch_layers],
        cost_estimate=pl.CostEstimate(flops=passes * size, bytes_accessed=4 * size, transcendentals=0),
        compiler_params=PARAMS,
        name=name,
    )


def per_device(states, shift, step_size):
    start = states[0]
    depth = start.shape[1]
    slabs, sections = lax.axis_size("gz"), lax.axis_size("tm")
    same_chip = [(i, i ^ 1) for i in range(slabs)]
    next_chip = [(i, (i + 1 if i % 2 else i - 1) % slabs) for i in range(slabs)]
    forth = [(i, (i + 1) % sections) for i in range(sections)]
    back = [((i + 1) % sections, i) for i in range(sections)]

    cross = lax.ppermute(start, "gz", next_chip)
    pairs = [[i, i + 1] for i in range(0, slabs, 2)]
    other = 1 - lax.axis_index("gz") % 2
    low = lax.all_gather(start[:2], "gz", axis_index_groups=pairs)
    high = lax.all_gather(start[2:], "gz", axis_index_groups=pairs)
    chip = jnp.concatenate([low[other], high[other]])
    following = lax.ppermute(start, "tm", back)
    own = kernel(copy_kernel, start, [VMEM], depth, name="stage")(start)
    partial = kernel(forward_cross_kernel, start, [VMEM] * 2, 7, (3, 2), "forward_cross")(own, cross)
    ends = kernel(forward_chip_kernel, start, [VMEM] * 3, depth, (4, 4, 4), "forward_chip")(own, chip, partial)
    ends, following = lax.optimization_barrier((ends, following))
    prior_ends = lax.ppermute(ends, "tm", forth)
    mismatch = kernel(compare_kernel, start, [SMEM, VMEM, VMEM], depth, (), "compare")(shift, ends, following)
    cross_mis = lax.ppermute(mismatch, "gz", next_chip)
    chip_mis = lax.ppermute(mismatch, "gz", same_chip)
    prior = kernel(carry_kernel, start, [SMEM, VMEM, VMEM], depth, (), "carry", 2)(shift, own, prior_ends)
    partial = kernel(adjoint_cross_kernel, start, [VMEM] * 2, 6, (4, 2), "adjoint_cross")(mismatch, cross_mis)
    updated = kernel(adjoint_chip_kernel, start, [SMEM] + [VMEM] * 7, depth, (4, 4, 4), "adjoint_chip")(
        step_size, own, chip, cross, mismatch, chip_mis, prior, partial
    )
    shown = kernel(copy_kernel, start, [VMEM], depth, name="publish")(mismatch)
    return updated[None], shown[None]


def solution(mesh):
    placed = P("tm", None, "gz", None, None)
    return jax.shard_map(
        per_device,
        mesh=mesh,
        in_specs=(placed, P(), P()),
        out_specs=(placed, placed),
        check_vma=False,
    )
```

```python
import jax
import jax.numpy as jnp
from jax import lax
from jax.experimental import pallas as pl
from jax.experimental.pallas import tpu as pltpu
from jax.sharding import PartitionSpec as P

SWEEPS = 3
TAU = 0.2
HALF_TAU = 0.5 * TAU
VISCOUS = 1.0
SCALE = 1.0 / (1.0 + 6.0 * VISCOUS)


def base_speed(shape):
    rows = shape[0]
    cell = lax.broadcasted_iota(jnp.int32, shape, 0).astype(jnp.float32)
    radius = 1.0 + (cell + 0.5) / rows
    return 0.2 + 0.6 / (radius * radius)


def lane_up(f):
    return pltpu.roll(f, f.shape[1] - 1, 1)


def lane_down(f):
    return pltpu.roll(f, 1, 1)


class Walls:
    def __init__(self, shape):
        row = lax.broadcasted_iota(jnp.int32, shape, 0)
        self.first = row == 0
        self.last = row == shape[0] - 1
        self.rows = shape[0]

    def up(self, f):
        return jnp.where(self.last, 0.0, pltpu.roll(f, self.rows - 1, 0))

    def down(self, f):
        return jnp.where(self.first, 0.0, pltpu.roll(f, 1, 0))


def place(layer, depth, odd):
    k = layer % depth
    return k + odd * (depth - 1 - 2 * k)


def layer_of(refs, field, layer, depth, odd):
    behind, own, ahead = refs
    ref = behind if layer < 0 else own if layer < depth else ahead
    return ref[field, place(layer, depth, odd)]


def in_plane(f, walls):
    return lane_up(f) + lane_down(f) + walls.up(f) + walls.down(f)


def explicit(at, put, layers, sign, walls, speed):
    for layer in layers:
        here = [at(f, layer) for f in range(4)]
        d_z = [at(f, layer + 1) - at(f, layer - 1) for f in range(4)]
        d_th = [lane_up(f) - lane_down(f) for f in here]
        d_r = [walls.up(f) - walls.down(f) for f in here]
        u, v, w, p = here
        by_th = HALF_TAU * (speed + v)
        by_r = HALF_TAU * u
        by_z = (HALF_TAU * sign) * w
        carried = [by_th * d_th[f] + by_r * d_r[f] + by_z * d_z[f] for f in range(3)]
        put(0, layer, u - (carried[0] + HALF_TAU * d_r[3]) + (2.0 * TAU) * speed * v)
        put(1, layer, v - (carried[1] + HALF_TAU * d_th[3]) - TAU * speed * u)
        put(2, layer, w - (carried[2] + (HALF_TAU * sign) * d_z[3]))
        put(3, layer, p - HALF_TAU * (d_r[0] + d_th[1] + sign * d_z[2]))


PAD = 8


class Slabs:
    def __init__(self, refs, depth, odd, walls):
        self.refs, self.depth, self.odd, self.walls = refs, depth, odd, walls

    def get(self, field, layer):
        return layer_of(self.refs, field, layer, self.depth, self.odd)

    def up(self, field, layer):
        return self.walls.up(self.get(field, layer))

    def down(self, field, layer):
        return self.walls.down(self.get(field, layer))


class Level:
    def __init__(self, *parts):
        self.parts = parts
        self.rows = parts[0][0].shape[2] - 2 * PAD

    def at(self, field, layer, first):
        for ref, low, high, start in self.parts:
            if low <= layer < high:
                return ref[field, start + layer - low, first : first + self.rows]

    def get(self, field, layer):
        return self.at(field, layer, PAD)

    def up(self, field, layer):
        return self.at(field, layer, PAD + 1)

    def down(self, field, layer):
        return self.at(field, layer, PAD - 1)

    def put(self, field, layer, value):
        for ref, low, high, start in self.parts:
            if low <= layer < high:
                ref[field, start + layer - low, PAD : PAD + self.rows] = value


def clear_pads(*refs):
    for ref in refs:
        fields, layers, rows, columns = ref.shape
        nothing = jnp.zeros((PAD, columns), jnp.float32)
        for f in range(fields):
            for k in range(layers):
                ref[f, k, :PAD] = nothing
                ref[f, k, rows - PAD :] = nothing


def neighbours(level, field, layer):
    here = level.get(field, layer)
    around = level.get(field, layer - 1) + level.get(field, layer + 1) + lane_up(here) + lane_down(here)
    return around + level.up(field, layer) + level.down(field, layer)


def facing(own, turned=0):
    depth = own.shape[1]
    odd = (lax.axis_index("gz") + turned) % 2
    return depth, odd, (1 - 2 * odd).astype(jnp.float32), Walls(own.shape[2:]), base_speed(own.shape[2:])


def forward_cross_kernel(own, cross, partial, force, first):
    depth, odd, sign, walls, speed = facing(own)

    def at(field, layer):
        return layer_of((cross, own, None), field, layer, depth, odd)

    clear_pads(partial, force, first)
    e = Level((force, -3, 0, 0), (partial, 0, depth - 1, 0))
    one = Level((first, -2, 0, 0), (partial, 0, 2, 3))
    two = Level((partial, -1, 1, 5))
    explicit(at, e.put, range(-3, depth - 1), sign, walls, speed)
    for f in range(4):
        for layer in range(-2, 2):
            one.put(f, layer, (e.get(f, layer) + neighbours(e, f, layer)) * SCALE)
        for layer in range(-1, 1):
            two.put(f, layer, (e.get(f, layer) + neighbours(one, f, layer)) * SCALE)


def forward_chip_kernel(own, chip, partial, ends, force, first, second):
    depth, odd, sign, walls, speed = facing(own)

    def at(field, layer):
        return layer_of((None, own, chip), field, layer, depth, odd)

    clear_pads(force, first, second)
    e = Level((partial, 0, depth - 1, 0), (force, depth - 1, depth + 3, 0))
    one = Level((partial, 0, 2, 3), (first, 2, depth + 2, 0))
    two = Level((partial, -1, 1, 5), (second, 1, depth + 1, 0))
    explicit(at, e.put, range(depth - 1, depth + 3), sign, walls, speed)
    for f in range(4):
        for layer in range(2, depth + 2):
            one.put(f, layer, (e.get(f, layer) + neighbours(e, f, layer)) * SCALE)
        for layer in range(1, depth + 1):
            two.put(f, layer, (e.get(f, layer) + neighbours(one, f, layer)) * SCALE)
        for layer in range(depth):
            total = e.get(f, layer) + neighbours(two, f, layer)
            ends[f, place(layer, depth, odd)] = total * SCALE


def turn(field, amount):
    return pltpu.roll(field, amount, 1)


def compare_kernel(shift, ends, following, mismatch):
    fields, depth, rows, columns = ends.shape
    last = lax.axis_index("tm") == lax.axis_size("tm") - 1
    amount = jnp.where(last, shift[0], 0)
    for f in range(fields):
        for k in range(depth):
            mismatch[f, k] = ends[f, k] - turn(following[f, k], amount)


def carry_kernel(shift, own, prior_ends, prior):
    fields, depth, rows, columns = own.shape
    is_first = lax.axis_index("tm") == 0
    amount = jnp.where(is_first, columns - shift[0], 0) % columns
    for f in range(fields):
        for k in range(depth):
            prior[f, k] = turn(prior_ends[f, k], amount) - own[f, k]


def adjoint_chip_kernel(own_mis, chip_mis, partial, first, second):
    depth, odd, sign, walls, speed = facing(own_mis, 1)

    c = Slabs((chip_mis, own_mis, None), depth, odd, walls)

    clear_pads(partial, first, second)
    one = Level((first, -3, 1, 0), (partial, 1, 3, 2))
    two = Level((second, -2, 0, 0), (partial, 0, 2, 4))
    total = Level((partial, -1, 1, 0))
    for f in range(4):
        for layer in range(-3, 3):
            one.put(f, layer, neighbours(c, f, layer) * SCALE)
        for layer in range(-2, 2):
            two.put(f, layer, neighbours(one, f, layer) * SCALE)
        for layer in range(-1, 1):
            last = neighbours(two, f, layer)
            total.put(f, layer, (c.get(f, layer) + one.get(f, layer) + two.get(f, layer) + last) * SCALE)


def adjoint_cross_kernel(step_size, own, chip, cross, own_mis, cross_mis, prior, partial, updated, cot, first, second):
    depth, odd, sign, walls, speed = facing(own, 1)

    def at(field, layer):
        return layer_of((chip, own, cross), field, layer, depth, odd)

    c = Slabs((None, own_mis, cross_mis), depth, odd, walls)

    clear_pads(cot, first, second)
    one = Level((partial, 1, 3, 2), (first, 3, depth + 3, 0))
    two = Level((partial, 0, 2, 4), (second, 2, depth + 2, 0))
    total = Level((partial, -1, 1, 0), (cot, 1, depth + 1, 0))
    for f in range(4):
        for layer in range(3, depth + 3):
            one.put(f, layer, neighbours(c, f, layer) * SCALE)
        for layer in range(2, depth + 2):
            two.put(f, layer, neighbours(one, f, layer) * SCALE)
        for layer in range(1, depth + 1):
            last = neighbours(two, f, layer)
            total.put(f, layer, (c.get(f, layer) + one.get(f, layer) + two.get(f, layer) + last) * SCALE)

    size = step_size[0]
    half = HALF_TAU

    def th(f):
        return lane_up(f) - lane_down(f)

    def rad(f):
        return walls.up(f) - walls.down(f)

    for layer in range(depth):
        here = [at(f, layer) for f in range(4)]
        u, v, w, p = here
        c0, c1, c2, c3 = (total.get(f, layer) for f in range(4))
        below = [total.get(f, layer - 1) for f in range(4)]
        above = [total.get(f, layer + 1) for f in range(4)]
        w_below, w_above = at(2, layer - 1), at(2, layer + 1)
        swirl = speed + v
        pull_r = c0 * rad(u) + c1 * rad(v) + c2 * rad(w)
        pull_th = c0 * th(u) + c1 * th(v) + c2 * th(w)
        pull_z = sum(x * (at(f, layer + 1) - at(f, layer - 1)) for f, x in ((0, c0), (1, c1), (2, c2)))
        axial = [w_above * above[f] - w_below * below[f] for f in range(3)]
        grads = [
            c0 + half * (th(swirl * c0) + rad(u * c0 + c3) + sign * axial[0] - pull_r) - TAU * speed * c1,
            c1
            + half * (th(swirl * c1 + c3) + rad(u * c1) + sign * axial[1] - pull_th)
            + (2.0 * TAU) * speed * c0,
            c2 + half * (th(swirl * c2) + rad(u * c2) + sign * (axial[2] + above[3] - below[3] - pull_z)),
            c3 + half * (total.up(0, layer) - total.down(0, layer) + th(c1) + sign * (above[2] - below[2])),
        ]
        to = place(layer, depth, odd)
        for f in range(4):
            updated[f, to] = here[f] - size * (grads[f] - prior[f, to])


def copy_kernel(source, own):
    for f in range(source.shape[0]):
        for k in range(source.shape[1]):
            own[f, k] = source[f, k]


VMEM = pl.BlockSpec(memory_space=pltpu.VMEM)
PARAMS = pltpu.CompilerParams(vmem_limit_bytes=16 * 2**20)
SMEM = pl.BlockSpec(memory_space=pltpu.SMEM)


def kernel(body, like, ins, out_layers, scratch_layers=(), name=None, passes=50, pad=0):
    fields, depth, rows, columns = like.shape
    size = fields * depth * rows * columns
    return pl.pallas_call(
        body,
        out_shape=jax.ShapeDtypeStruct((fields, out_layers, rows + 2 * pad, columns), jnp.float32),
        in_specs=ins,
        out_specs=VMEM,
        scratch_shapes=[pltpu.VMEM((fields, n, rows + 2 * PAD, columns), jnp.float32) for n in scratch_layers],
        cost_estimate=pl.CostEstimate(flops=passes * size, bytes_accessed=4 * size, transcendentals=0),
        compiler_params=PARAMS,
        name=name,
    )


def per_device(states, shift, step_size):
    start = states[0]
    depth = start.shape[1]
    slabs, sections = lax.axis_size("gz"), lax.axis_size("tm")
    next_chip = [(i, (i + 1 if i % 2 else i - 1) % slabs) for i in range(slabs)]
    forth = [(i, (i + 1) % sections) for i in range(sections)]
    back = [((i + 1) % sections, i) for i in range(sections)]

    cross = lax.ppermute(start, "gz", next_chip)
    pairs = [[i, i + 1] for i in range(0, slabs, 2)]
    other = 1 - lax.axis_index("gz") % 2
    low = lax.all_gather(start[:2], "gz", axis_index_groups=pairs)
    high = lax.all_gather(start[2:], "gz", axis_index_groups=pairs)
    chip = jnp.concatenate([low[other], high[other]])
    following = lax.ppermute(start, "tm", back)
    own = kernel(copy_kernel, start, [VMEM], depth, name="stage")(start)
    partial = kernel(forward_cross_kernel, start, [VMEM] * 2, 7, (3, 2), "forward_cross", pad=PAD)(own, cross)
    ends = kernel(forward_chip_kernel, start, [VMEM] * 3, depth, (4, 4, 4), "forward_chip")(own, chip, partial)
    ends, following = lax.optimization_barrier((ends, following))
    prior_ends = lax.ppermute(ends, "tm", forth)
    mismatch = kernel(compare_kernel, start, [SMEM, VMEM, VMEM], depth, (), "compare")(shift, ends, following)
    cross_mis = lax.ppermute(mismatch, "gz", next_chip)
    low = lax.all_gather(mismatch[:2], "gz", axis_index_groups=pairs)
    high = lax.all_gather(mismatch[2:], "gz", axis_index_groups=pairs)
    chip_mis = jnp.concatenate([low[other], high[other]])
    prior = kernel(carry_kernel, start, [SMEM, VMEM, VMEM], depth, (), "carry", 2)(shift, own, prior_ends)
    partial = kernel(adjoint_chip_kernel, start, [VMEM] * 2, 6, (4, 2), "adjoint_chip", pad=PAD)(mismatch, chip_mis)
    updated = kernel(adjoint_cross_kernel, start, [SMEM] + [VMEM] * 7, depth, (4, 4, 4), "adjoint_cross")(
        step_size, own, chip, cross, mismatch, cross_mis, prior, partial
    )
    shown = kernel(copy_kernel, start, [VMEM], depth, name="publish")(mismatch)
    return updated[None], shown[None]


def solution(mesh):
    placed = P("tm", None, "gz", None, None)
    return jax.shard_map(
        per_device,
        mesh=mesh,
        in_specs=(placed, P(), P()),
        out_specs=(placed, placed),
        check_vma=False,
    )
```

```python
import jax
import jax.numpy as jnp
from jax import lax
from jax.experimental import pallas as pl
from jax.experimental.pallas import tpu as pltpu
from jax.sharding import PartitionSpec as P

SWEEPS = 3
TAU = 0.2
HALF_TAU = 0.5 * TAU
VISCOUS = 1.0
SCALE = 1.0 / (1.0 + 6.0 * VISCOUS)


def base_speed(shape):
    rows = shape[0]
    cell = lax.broadcasted_iota(jnp.int32, shape, 0).astype(jnp.float32)
    radius = 1.0 + (cell + 0.5) / rows
    return 0.2 + 0.6 / (radius * radius)


def lane_up(f):
    return pltpu.roll(f, f.shape[1] - 1, 1)


def lane_down(f):
    return pltpu.roll(f, 1, 1)


class Walls:
    def __init__(self, shape):
        row = lax.broadcasted_iota(jnp.int32, shape, 0)
        self.first = row == 0
        self.last = row == shape[0] - 1
        self.rows = shape[0]

    def up(self, f):
        return jnp.where(self.last, 0.0, pltpu.roll(f, self.rows - 1, 0))

    def down(self, f):
        return jnp.where(self.first, 0.0, pltpu.roll(f, 1, 0))


def place(layer, depth, odd):
    k = layer % depth
    return k + odd * (depth - 1 - 2 * k)


def layer_of(refs, field, layer, depth, odd):
    behind, own, ahead = refs
    ref = behind if layer < 0 else own if layer < depth else ahead
    return ref[field, place(layer, depth, odd)]


def in_plane(f, walls):
    return lane_up(f) + lane_down(f) + walls.up(f) + walls.down(f)


CHUNK = 16


def explicit(state, put, layers, sign, speed):
    rows, columns = speed.shape
    edges = Walls((CHUNK, columns))
    for layer in layers:
        for row in range(0, rows, CHUNK):
            b = speed[row : row + CHUNK]
            u, v, w, p = (state.cut(f, layer, row, CHUNK) for f in range(4))
            by_th = HALF_TAU * (b + v)
            by_r = HALF_TAU * u
            by_z = (HALF_TAU * sign) * w

            def carried(f, here):
                d_z = state.cut(f, layer + 1, row, CHUNK) - state.cut(f, layer - 1, row, CHUNK)
                d_th = lane_up(here) - lane_down(here)
                d_r = state.across(f, layer, row, CHUNK, edges)
                return d_r, d_th, d_z, by_th * d_th + by_r * d_r + by_z * d_z

            p_r = state.across(3, layer, row, CHUNK, edges)
            u_r, _, _, moved = carried(0, u)
            put(0, layer, u - (moved + HALF_TAU * p_r) + (2.0 * TAU) * b * v, row)
            p_th = lane_up(p) - lane_down(p)
            _, v_th, _, moved = carried(1, v)
            put(1, layer, v - (moved + HALF_TAU * p_th) - TAU * b * u, row)
            p_z = state.cut(3, layer + 1, row, CHUNK) - state.cut(3, layer - 1, row, CHUNK)
            _, _, w_z, moved = carried(2, w)
            put(2, layer, w - (moved + (HALF_TAU * sign) * p_z), row)
            put(3, layer, p - HALF_TAU * (u_r + v_th + sign * w_z), row)


PAD = 8


class Slabs:
    def __init__(self, refs, depth, odd, walls):
        self.refs, self.depth, self.odd, self.walls = refs, depth, odd, walls

    def get(self, field, layer):
        return layer_of(self.refs, field, layer, self.depth, self.odd)

    def cut(self, field, layer, row, count):
        behind, own, ahead = self.refs
        ref = behind if layer < 0 else own if layer < self.depth else ahead
        return ref[field, place(layer, self.depth, self.odd), row : row + count]

    def across(self, field, layer, row, count, edges):
        here = self.cut(field, layer, row, count)
        total = self.refs[1].shape[2]
        above = self.cut(field, layer, row + 1, count) if row + count < total else edges.up(here)
        below = self.cut(field, layer, row - 1, count) if row else edges.down(here)
        return above - below

    def up(self, field, layer):
        return self.walls.up(self.get(field, layer))

    def down(self, field, layer):
        return self.walls.down(self.get(field, layer))


class Level:
    def __init__(self, *parts):
        self.parts = parts
        self.rows = parts[0][0].shape[2] - 2 * PAD

    def at(self, field, layer, first, count=None):
        for ref, low, high, start in self.parts:
            if low <= layer < high:
                return ref[field, start + layer - low, first : first + (count or self.rows)]

    def get(self, field, layer):
        return self.at(field, layer, PAD)

    def up(self, field, layer):
        return self.at(field, layer, PAD + 1)

    def down(self, field, layer):
        return self.at(field, layer, PAD - 1)

    def put(self, field, layer, value, row=0):
        for ref, low, high, start in self.parts:
            if low <= layer < high:
                ref[field, start + layer - low, PAD + row : PAD + row + value.shape[0]] = value


def clear_pads(*refs):
    for ref in refs:
        fields, layers, rows, columns = ref.shape
        nothing = jnp.zeros((PAD, columns), jnp.float32)
        for f in range(fields):
            for k in range(layers):
                ref[f, k, :PAD] = nothing
                ref[f, k, rows - PAD :] = nothing


def neighbours(level, field, layer):
    here = level.get(field, layer)
    around = level.get(field, layer - 1) + level.get(field, layer + 1) + lane_up(here) + lane_down(here)
    return around + level.up(field, layer) + level.down(field, layer)


def facing(own, turned=0):
    depth = own.shape[1]
    odd = (lax.axis_index("gz") + turned) % 2
    return depth, odd, (1 - 2 * odd).astype(jnp.float32), Walls(own.shape[2:]), base_speed(own.shape[2:])


def forward_cross_kernel(own, cross, partial, force, first):
    depth, odd, sign, walls, speed = facing(own)

    state = Slabs((cross, own, None), depth, odd, walls)

    clear_pads(partial, force, first)
    e = Level((force, -3, 0, 0), (partial, 0, depth - 1, 0))
    one = Level((first, -2, 0, 0), (partial, 0, 2, 3))
    two = Level((partial, -1, 1, 5))
    explicit(state, e.put, range(-3, depth - 1), sign, speed)
    for f in range(4):
        for layer in range(-2, 2):
            one.put(f, layer, (e.get(f, layer) + neighbours(e, f, layer)) * SCALE)
        for layer in range(-1, 1):
            two.put(f, layer, (e.get(f, layer) + neighbours(one, f, layer)) * SCALE)


def forward_chip_kernel(own, chip, partial, ends, force, first, second):
    depth, odd, sign, walls, speed = facing(own)

    state = Slabs((None, own, chip), depth, odd, walls)

    clear_pads(force, first, second)
    e = Level((partial, 0, depth - 1, 0), (force, depth - 1, depth + 3, 0))
    one = Level((partial, 0, 2, 3), (first, 2, depth + 2, 0))
    two = Level((partial, -1, 1, 5), (second, 1, depth + 1, 0))
    explicit(state, e.put, range(depth - 1, depth + 3), sign, speed)
    for f in range(4):
        for layer in range(2, depth + 2):
            one.put(f, layer, (e.get(f, layer) + neighbours(e, f, layer)) * SCALE)
        for layer in range(1, depth + 1):
            two.put(f, layer, (e.get(f, layer) + neighbours(one, f, layer)) * SCALE)
        for layer in range(depth):
            total = e.get(f, layer) + neighbours(two, f, layer)
            ends[f, place(layer, depth, odd)] = total * SCALE


def turn(field, amount):
    return pltpu.roll(field, amount, 1)


def compare_kernel(shift, ends, following, mismatch):
    fields, depth, rows, columns = ends.shape
    last = lax.axis_index("tm") == lax.axis_size("tm") - 1
    amount = jnp.where(last, shift[0], 0)
    for f in range(fields):
        for k in range(depth):
            mismatch[f, k] = ends[f, k] - turn(following[f, k], amount)


def carry_kernel(shift, own, prior_ends, prior):
    fields, depth, rows, columns = own.shape
    is_first = lax.axis_index("tm") == 0
    amount = jnp.where(is_first, columns - shift[0], 0) % columns
    for f in range(fields):
        for k in range(depth):
            prior[f, k] = turn(prior_ends[f, k], amount) - own[f, k]


def adjoint_chip_kernel(own_mis, chip_mis, partial, first, second):
    depth, odd, sign, walls, speed = facing(own_mis, 1)

    c = Slabs((chip_mis, own_mis, None), depth, odd, walls)

    clear_pads(partial, first, second)
    one = Level((first, -3, 1, 0), (partial, 1, 3, 2))
    two = Level((second, -2, 0, 0), (partial, 0, 2, 4))
    total = Level((partial, -1, 1, 0))
    for f in range(4):
        for layer in range(-3, 3):
            one.put(f, layer, neighbours(c, f, layer) * SCALE)
        for layer in range(-2, 2):
            two.put(f, layer, neighbours(one, f, layer) * SCALE)
        for layer in range(-1, 1):
            last = neighbours(two, f, layer)
            total.put(f, layer, (c.get(f, layer) + one.get(f, layer) + two.get(f, layer) + last) * SCALE)


def slopes_kernel(own, chip, cross, slopes):
    depth, odd, sign, walls, speed = facing(own, 1)
    state = Slabs((chip, own, cross), depth, odd, walls)
    for layer in range(depth):
        for f in range(3):
            here = state.get(f, layer)
            slopes[f, layer] = lane_up(here) - lane_down(here)
            slopes[3 + f, layer] = walls.up(here) - walls.down(here)
            slopes[6 + f, layer] = state.get(f, layer + 1) - state.get(f, layer - 1)


def adjoint_cross_kernel(step_size, own, chip, cross, own_mis, cross_mis, prior, slopes, partial, updated, cot, first, second, flux):
    depth, odd, sign, walls, speed = facing(own, 1)

    state = Slabs((chip, own, cross), depth, odd, walls)
    c = Slabs((None, own_mis, cross_mis), depth, odd, walls)

    clear_pads(cot, first, second, flux)
    one = Level((partial, 1, 3, 2), (first, 3, depth + 3, 0))
    two = Level((partial, 0, 2, 4), (second, 2, depth + 2, 0))
    total = Level((partial, -1, 1, 0), (cot, 1, depth + 1, 0))
    for f in range(4):
        for layer in range(3, depth + 3):
            one.put(f, layer, neighbours(c, f, layer) * SCALE)
        for layer in range(2, depth + 2):
            two.put(f, layer, neighbours(one, f, layer) * SCALE)
        for layer in range(1, depth + 1):
            last = neighbours(two, f, layer)
            total.put(f, layer, (c.get(f, layer) + one.get(f, layer) + two.get(f, layer) + last) * SCALE)

    size = step_size[0]
    half = HALF_TAU
    moving = Level((flux, 0, depth, 0))
    for layer in range(depth):
        u = state.get(0, layer)
        moving.put(0, layer, u * total.get(0, layer) + total.get(3, layer))
        moving.put(1, layer, u * total.get(1, layer))
        moving.put(2, layer, u * total.get(2, layer))

    def th(f):
        return lane_up(f) - lane_down(f)

    for layer in range(depth):
        to = place(layer, depth, odd)
        for row in range(0, own.shape[2], CHUNK):
            at = PAD + row

            def rad(level, f):
                return level.at(f, layer, at + 1, CHUNK) - level.at(f, layer, at - 1, CHUNK)

            def slope(f):
                return slopes[f, layer, row : row + CHUNK]

            def write(f, here, grad):
                updated[f, to, row : row + CHUNK] = here - size * (grad - prior[f, to, row : row + CHUNK])

            u, v, w, p = (state.cut(f, layer, row, CHUNK) for f in range(4))
            b = speed[row : row + CHUNK]
            c0, c1, c2, c3 = (total.at(f, layer, at, CHUNK) for f in range(4))
            below = [total.at(f, layer - 1, at, CHUNK) for f in range(4)]
            above = [total.at(f, layer + 1, at, CHUNK) for f in range(4)]
            w_below, w_above = state.cut(2, layer - 1, row, CHUNK), state.cut(2, layer + 1, row, CHUNK)
            swirl = b + v
            axial = [w_above * above[f] - w_below * below[f] for f in range(3)]
            pull = c0 * slope(3) + c1 * slope(4) + c2 * slope(5)
            step = half * (th(swirl * c0) + rad(moving, 0) + sign * axial[0] - pull)
            write(0, u, c0 + step - TAU * b * c1)
            pull = c0 * slope(0) + c1 * slope(1) + c2 * slope(2)
            step = half * (th(swirl * c1 + c3) + rad(moving, 1) + sign * axial[1] - pull)
            write(1, v, c1 + step + (2.0 * TAU) * b * c0)
            pull = c0 * slope(6) + c1 * slope(7) + c2 * slope(8)
            step = half * (th(swirl * c2) + rad(moving, 2) + sign * (axial[2] + above[3] - below[3] - pull))
            write(2, w, c2 + step)
            write(3, p, c3 + half * (rad(total, 0) + th(c1) + sign * (above[2] - below[2])))


def copy_kernel(source, own):
    for f in range(source.shape[0]):
        for k in range(source.shape[1]):
            own[f, k] = source[f, k]


VMEM = pl.BlockSpec(memory_space=pltpu.VMEM)
PARAMS = pltpu.CompilerParams(vmem_limit_bytes=16 * 2**20)
SMEM = pl.BlockSpec(memory_space=pltpu.SMEM)


def kernel(body, like, ins, out_layers, scratch_layers=(), name=None, passes=50, pad=0, fields=4):
    _, depth, rows, columns = like.shape
    size = fields * depth * rows * columns
    return pl.pallas_call(
        body,
        out_shape=jax.ShapeDtypeStruct((fields, out_layers, rows + 2 * pad, columns), jnp.float32),
        in_specs=ins,
        out_specs=VMEM,
        scratch_shapes=[pltpu.VMEM((4, n, rows + 2 * PAD, columns), jnp.float32) for n in scratch_layers],
        cost_estimate=pl.CostEstimate(flops=passes * size, bytes_accessed=4 * size, transcendentals=0),
        compiler_params=PARAMS,
        name=name,
    )


def per_device(states, shift, step_size):
    start = states[0]
    depth = start.shape[1]
    slabs, sections = lax.axis_size("gz"), lax.axis_size("tm")
    next_chip = [(i, (i + 1 if i % 2 else i - 1) % slabs) for i in range(slabs)]
    forth = [(i, (i + 1) % sections) for i in range(sections)]
    back = [((i + 1) % sections, i) for i in range(sections)]

    cross = lax.ppermute(start, "gz", next_chip)
    pairs = [[i, i + 1] for i in range(0, slabs, 2)]
    other = 1 - lax.axis_index("gz") % 2
    low = lax.all_gather(start[:2], "gz", axis_index_groups=pairs)
    high = lax.all_gather(start[2:], "gz", axis_index_groups=pairs)
    chip = jnp.concatenate([low[other], high[other]])
    following = lax.ppermute(start, "tm", back)
    own = kernel(copy_kernel, start, [VMEM], depth, name="stage")(start)
    partial = kernel(forward_cross_kernel, start, [VMEM] * 2, 7, (3, 2), "forward_cross", pad=PAD)(own, cross)
    ends = kernel(forward_chip_kernel, start, [VMEM] * 3, depth, (4, 4, 4), "forward_chip")(own, chip, partial)
    ends, following = lax.optimization_barrier((ends, following))
    prior_ends = lax.ppermute(ends, "tm", forth)
    mismatch = kernel(compare_kernel, start, [SMEM, VMEM, VMEM], depth, (), "compare")(shift, ends, following)
    cross_mis = lax.ppermute(mismatch, "gz", next_chip)
    low = lax.all_gather(mismatch[:2], "gz", axis_index_groups=pairs)
    high = lax.all_gather(mismatch[2:], "gz", axis_index_groups=pairs)
    chip_mis = jnp.concatenate([low[other], high[other]])
    prior = kernel(carry_kernel, start, [SMEM, VMEM, VMEM], depth, (), "carry", 2)(shift, own, prior_ends)
    partial = kernel(adjoint_chip_kernel, start, [VMEM] * 2, 6, (4, 2), "adjoint_chip", pad=PAD)(mismatch, chip_mis)
    slopes = kernel(slopes_kernel, start, [VMEM] * 3, depth, (), "slopes", fields=9)(own, chip, cross)
    updated = kernel(adjoint_cross_kernel, start, [SMEM] + [VMEM] * 8, depth, (4, 4, 4, depth), "adjoint_cross")(
        step_size, own, chip, cross, mismatch, cross_mis, prior, slopes, partial
    )
    shown = kernel(copy_kernel, start, [VMEM], depth, name="publish")(mismatch)
    return updated[None], shown[None]


def solution(mesh):
    placed = P("tm", None, "gz", None, None)
    return jax.shard_map(
        per_device,
        mesh=mesh,
        in_specs=(placed, P(), P()),
        out_specs=(placed, placed),
        check_vma=False,
    )
```

```python
import jax
import jax.numpy as jnp
from jax import lax
from jax.experimental import pallas as pl
from jax.experimental.pallas import tpu as pltpu
from jax.sharding import PartitionSpec as P

SWEEPS = 3
TAU = 0.2
HALF_TAU = 0.5 * TAU
VISCOUS = 1.0
SCALE = 1.0 / (1.0 + 6.0 * VISCOUS)


def base_speed(shape):
    rows = shape[0]
    cell = lax.broadcasted_iota(jnp.int32, shape, 0).astype(jnp.float32)
    radius = 1.0 + (cell + 0.5) / rows
    return 0.2 + 0.6 / (radius * radius)


def lane_up(f):
    return pltpu.roll(f, f.shape[1] - 1, 1)


def lane_down(f):
    return pltpu.roll(f, 1, 1)


class Walls:
    def __init__(self, shape):
        row = lax.broadcasted_iota(jnp.int32, shape, 0)
        self.first = row == 0
        self.last = row == shape[0] - 1
        self.rows = shape[0]

    def up(self, f):
        return jnp.where(self.last, 0.0, pltpu.roll(f, self.rows - 1, 0))

    def down(self, f):
        return jnp.where(self.first, 0.0, pltpu.roll(f, 1, 0))


def place(layer, depth, odd):
    k = layer % depth
    return k + odd * (depth - 1 - 2 * k)


def layer_of(refs, field, layer, depth, odd):
    behind, own, ahead = refs
    ref = behind if layer < 0 else own if layer < depth else ahead
    return ref[field, place(layer, depth, odd)]


def in_plane(f, walls):
    return lane_up(f) + lane_down(f) + walls.up(f) + walls.down(f)


CHUNK = 8


def explicit(state, put, layers, sign, speed):
    rows, columns = speed.shape
    edges = Walls((CHUNK, columns))
    for layer in layers:
        for row in range(0, rows, CHUNK):
            b = speed[row : row + CHUNK]
            u, v, w, p = (state.cut(f, layer, row, CHUNK) for f in range(4))
            by_th = HALF_TAU * (b + v)
            by_r = HALF_TAU * u
            by_z = (HALF_TAU * sign) * w

            def carried(f, here):
                d_z = state.cut(f, layer + 1, row, CHUNK) - state.cut(f, layer - 1, row, CHUNK)
                d_th = lane_up(here) - lane_down(here)
                d_r = state.across(f, layer, row, CHUNK, edges)
                return d_r, d_th, d_z, by_th * d_th + by_r * d_r + by_z * d_z

            p_r = state.across(3, layer, row, CHUNK, edges)
            u_r, _, _, moved = carried(0, u)
            put(0, layer, u - (moved + HALF_TAU * p_r) + (2.0 * TAU) * b * v, row)
            p_th = lane_up(p) - lane_down(p)
            _, v_th, _, moved = carried(1, v)
            put(1, layer, v - (moved + HALF_TAU * p_th) - TAU * b * u, row)
            p_z = state.cut(3, layer + 1, row, CHUNK) - state.cut(3, layer - 1, row, CHUNK)
            _, _, w_z, moved = carried(2, w)
            put(2, layer, w - (moved + (HALF_TAU * sign) * p_z), row)
            put(3, layer, p - HALF_TAU * (u_r + v_th + sign * w_z), row)


PAD = 8


class Slabs:
    def __init__(self, refs, depth, odd, walls):
        self.refs, self.depth, self.odd, self.walls = refs, depth, odd, walls

    def get(self, field, layer):
        return layer_of(self.refs, field, layer, self.depth, self.odd)

    def cut(self, field, layer, row, count):
        behind, own, ahead = self.refs
        ref = behind if layer < 0 else own if layer < self.depth else ahead
        return ref[field, place(layer, self.depth, self.odd), row : row + count]

    def across(self, field, layer, row, count, edges):
        here = self.cut(field, layer, row, count)
        total = self.refs[1].shape[2]
        above = self.cut(field, layer, row + 1, count) if row + count < total else edges.up(here)
        below = self.cut(field, layer, row - 1, count) if row else edges.down(here)
        return above - below

    def up(self, field, layer):
        return self.walls.up(self.get(field, layer))

    def down(self, field, layer):
        return self.walls.down(self.get(field, layer))


class Level:
    def __init__(self, *parts):
        self.parts = parts
        self.rows = parts[0][0].shape[2] - 2 * PAD

    def at(self, field, layer, first, count=None):
        for ref, low, high, start in self.parts:
            if low <= layer < high:
                return ref[field, start + layer - low, first : first + (count or self.rows)]

    def get(self, field, layer):
        return self.at(field, layer, PAD)

    def up(self, field, layer):
        return self.at(field, layer, PAD + 1)

    def down(self, field, layer):
        return self.at(field, layer, PAD - 1)

    def put(self, field, layer, value, row=0):
        for ref, low, high, start in self.parts:
            if low <= layer < high:
                ref[field, start + layer - low, PAD + row : PAD + row + value.shape[0]] = value


def clear_pads(*refs):
    for ref in refs:
        fields, layers, rows, columns = ref.shape
        nothing = jnp.zeros((PAD, columns), jnp.float32)
        for f in range(fields):
            for k in range(layers):
                ref[f, k, :PAD] = nothing
                ref[f, k, rows - PAD :] = nothing


def neighbours(level, field, layer):
    here = level.get(field, layer)
    around = level.get(field, layer - 1) + level.get(field, layer + 1) + lane_up(here) + lane_down(here)
    return around + level.up(field, layer) + level.down(field, layer)


def facing(own, turned=0):
    depth = own.shape[1]
    odd = (lax.axis_index("gz") + turned) % 2
    return depth, odd, (1 - 2 * odd).astype(jnp.float32), Walls(own.shape[2:]), base_speed(own.shape[2:])


def forward_cross_kernel(own, cross, partial, force, first):
    depth, odd, sign, walls, speed = facing(own)

    state = Slabs((cross, own, None), depth, odd, walls)

    clear_pads(partial, force, first)
    e = Level((force, -3, 0, 0), (partial, 0, depth - 1, 0))
    one = Level((first, -2, 0, 0), (partial, 0, 2, 3))
    two = Level((partial, -1, 1, 5))
    explicit(state, e.put, range(-3, depth - 1), sign, speed)
    for f in range(4):
        for layer in range(-2, 2):
            one.put(f, layer, (e.get(f, layer) + neighbours(e, f, layer)) * SCALE)
        for layer in range(-1, 1):
            two.put(f, layer, (e.get(f, layer) + neighbours(one, f, layer)) * SCALE)


def forward_chip_kernel(own, chip, partial, ends, force, first, second):
    depth, odd, sign, walls, speed = facing(own)

    state = Slabs((None, own, chip), depth, odd, walls)

    clear_pads(force, first, second)
    e = Level((partial, 0, depth - 1, 0), (force, depth - 1, depth + 3, 0))
    one = Level((partial, 0, 2, 3), (first, 2, depth + 2, 0))
    two = Level((partial, -1, 1, 5), (second, 1, depth + 1, 0))
    explicit(state, e.put, range(depth - 1, depth + 3), sign, speed)
    for f in range(4):
        for layer in range(2, depth + 2):
            one.put(f, layer, (e.get(f, layer) + neighbours(e, f, layer)) * SCALE)
        for layer in range(1, depth + 1):
            two.put(f, layer, (e.get(f, layer) + neighbours(one, f, layer)) * SCALE)
        for layer in range(depth):
            total = e.get(f, layer) + neighbours(two, f, layer)
            ends[f, place(layer, depth, odd)] = total * SCALE


def turn(field, amount):
    return pltpu.roll(field, amount, 1)


def compare_kernel(shift, ends, following, mismatch):
    fields, depth, rows, columns = ends.shape
    last = lax.axis_index("tm") == lax.axis_size("tm") - 1
    amount = jnp.where(last, shift[0], 0)
    for f in range(fields):
        for k in range(depth):
            mismatch[f, k] = ends[f, k] - turn(following[f, k], amount)


def carry_kernel(shift, own, prior_ends, prior):
    fields, depth, rows, columns = own.shape
    is_first = lax.axis_index("tm") == 0
    amount = jnp.where(is_first, columns - shift[0], 0) % columns
    for f in range(fields):
        for k in range(depth):
            prior[f, k] = turn(prior_ends[f, k], amount) - own[f, k]


def adjoint_chip_kernel(own_mis, chip_mis, partial, first, second):
    depth, odd, sign, walls, speed = facing(own_mis, 1)

    c = Slabs((chip_mis, own_mis, None), depth, odd, walls)

    clear_pads(partial, first, second)
    one = Level((first, -3, 1, 0), (partial, 1, 3, 2))
    two = Level((second, -2, 0, 0), (partial, 0, 2, 4))
    total = Level((partial, -1, 1, 0))
    for f in range(4):
        for layer in range(-3, 3):
            one.put(f, layer, neighbours(c, f, layer) * SCALE)
        for layer in range(-2, 2):
            two.put(f, layer, neighbours(one, f, layer) * SCALE)
        for layer in range(-1, 1):
            last = neighbours(two, f, layer)
            total.put(f, layer, (c.get(f, layer) + one.get(f, layer) + two.get(f, layer) + last) * SCALE)


def slopes_kernel(own, chip, cross, slopes):
    depth, odd, sign, walls, speed = facing(own, 1)
    state = Slabs((chip, own, cross), depth, odd, walls)
    for layer in range(depth):
        for f in range(3):
            here = state.get(f, layer)
            slopes[f, layer] = lane_up(here) - lane_down(here)
            slopes[3 + f, layer] = walls.up(here) - walls.down(here)
            slopes[6 + f, layer] = state.get(f, layer + 1) - state.get(f, layer - 1)


def adjoint_cross_kernel(step_size, own, chip, cross, own_mis, cross_mis, prior, slopes, partial, updated, cot, first, second, flux, done, sems):
    depth, odd, sign, walls, speed = facing(own, 1)

    state = Slabs((chip, own, cross), depth, odd, walls)
    c = Slabs((None, own_mis, cross_mis), depth, odd, walls)

    clear_pads(cot, first, second, flux)
    one = Level((partial, 1, 3, 2), (first, 3, depth + 3, 0))
    two = Level((partial, 0, 2, 4), (second, 2, depth + 2, 0))
    total = Level((partial, -1, 1, 0), (cot, 1, depth + 1, 0))
    size = step_size[0]
    half = HALF_TAU
    moving = Level((flux, 0, depth, 0))
    def advance(layer):
        for f in range(4):
            one.put(f, layer + 3, neighbours(c, f, layer + 3) * SCALE)
            two.put(f, layer + 2, neighbours(one, f, layer + 2) * SCALE)
            near = layer + 1
            last = neighbours(two, f, near)
            total.put(f, near, (c.get(f, near) + one.get(f, near) + two.get(f, near) + last) * SCALE)
        u = state.get(0, layer)
        moving.put(0, layer, u * total.get(0, layer) + total.get(3, layer))
        moving.put(1, layer, u * total.get(1, layer))
        moving.put(2, layer, u * total.get(2, layer))

    def th(f):
        return lane_up(f) - lane_down(f)

    copies = []
    for layer in range(depth):
        advance(layer)
        to = place(layer, depth, odd)
        for row in range(0, own.shape[2], CHUNK):
            at = PAD + row

            def rad(level, f):
                return level.at(f, layer, at + 1, CHUNK) - level.at(f, layer, at - 1, CHUNK)

            def slope(f):
                return slopes[f, layer, row : row + CHUNK]

            def write(f, here, grad):
                done[f, layer, row : row + CHUNK] = here - size * (grad - prior[f, to, row : row + CHUNK])

            u, v, w, p = (state.cut(f, layer, row, CHUNK) for f in range(4))
            b = speed[row : row + CHUNK]
            c0, c1, c2, c3 = (total.at(f, layer, at, CHUNK) for f in range(4))
            below = [total.at(f, layer - 1, at, CHUNK) for f in range(4)]
            above = [total.at(f, layer + 1, at, CHUNK) for f in range(4)]
            w_below, w_above = state.cut(2, layer - 1, row, CHUNK), state.cut(2, layer + 1, row, CHUNK)
            swirl = b + v
            axial = [w_above * above[f] - w_below * below[f] for f in range(3)]
            pull = c0 * slope(3) + c1 * slope(4) + c2 * slope(5)
            step = half * (th(swirl * c0) + rad(moving, 0) + sign * axial[0] - pull)
            write(0, u, c0 + step - TAU * b * c1)
            pull = c0 * slope(0) + c1 * slope(1) + c2 * slope(2)
            step = half * (th(swirl * c1 + c3) + rad(moving, 1) + sign * axial[1] - pull)
            write(1, v, c1 + step + (2.0 * TAU) * b * c0)
            pull = c0 * slope(6) + c1 * slope(7) + c2 * slope(8)
            step = half * (th(swirl * c2) + rad(moving, 2) + sign * (axial[2] + above[3] - below[3] - pull))
            write(2, w, c2 + step)
            write(3, p, c3 + half * (rad(total, 0) + th(c1) + sign * (above[2] - below[2])))
        for f in range(4):
            source = done.at[f, layer, pl.ds(0, own.shape[2])]
            copies.append(pltpu.make_async_copy(source, updated.at[f, to], sems.at[f, layer]))
            copies[-1].start()
    for copy in copies:
        copy.wait()


def copy_kernel(source, own):
    for f in range(source.shape[0]):
        for k in range(source.shape[1]):
            own[f, k] = source[f, k]


VMEM = pl.BlockSpec(memory_space=pltpu.VMEM)
PARAMS = pltpu.CompilerParams(vmem_limit_bytes=16 * 2**20)
HBM = pl.BlockSpec(memory_space=pltpu.HBM)
SMEM = pl.BlockSpec(memory_space=pltpu.SMEM)


def kernel(body, like, ins, out_layers, scratch_layers=(), name=None, passes=50, pad=0, fields=4, out=VMEM, extra=()):
    _, depth, rows, columns = like.shape
    size = fields * depth * rows * columns
    return pl.pallas_call(
        body,
        out_shape=jax.ShapeDtypeStruct((fields, out_layers, rows + 2 * pad, columns), jnp.float32),
        in_specs=ins,
        out_specs=out,
        scratch_shapes=[pltpu.VMEM((4, n, rows + 2 * PAD, columns), jnp.float32) for n in scratch_layers] + list(extra),
        cost_estimate=pl.CostEstimate(flops=passes * size, bytes_accessed=4 * size, transcendentals=0),
        compiler_params=PARAMS,
        name=name,
    )


def per_device(states, shift, step_size):
    start = states[0]
    depth = start.shape[1]
    slabs, sections = lax.axis_size("gz"), lax.axis_size("tm")
    next_chip = [(i, (i + 1 if i % 2 else i - 1) % slabs) for i in range(slabs)]
    forth = [(i, (i + 1) % sections) for i in range(sections)]
    back = [((i + 1) % sections, i) for i in range(sections)]

    cross = lax.ppermute(start, "gz", next_chip)
    pairs = [[i, i + 1] for i in range(0, slabs, 2)]
    other = 1 - lax.axis_index("gz") % 2
    low = lax.all_gather(start[:2], "gz", axis_index_groups=pairs)
    high = lax.all_gather(start[2:], "gz", axis_index_groups=pairs)
    chip = jnp.concatenate([low[other], high[other]])
    following = lax.ppermute(start, "tm", back)
    own = kernel(copy_kernel, start, [VMEM], depth, name="stage")(start)
    partial = kernel(forward_cross_kernel, start, [VMEM] * 2, 7, (3, 2), "forward_cross", pad=PAD)(own, cross)
    ends = kernel(forward_chip_kernel, start, [VMEM] * 3, depth, (4, 4, 4), "forward_chip")(own, chip, partial)
    ends, following = lax.optimization_barrier((ends, following))
    prior_ends = lax.ppermute(ends, "tm", forth)
    mismatch = kernel(compare_kernel, start, [SMEM, VMEM, VMEM], depth, (), "compare")(shift, ends, following)
    cross_mis = lax.ppermute(mismatch, "gz", next_chip)
    low = lax.all_gather(mismatch[:2], "gz", axis_index_groups=pairs)
    high = lax.all_gather(mismatch[2:], "gz", axis_index_groups=pairs)
    chip_mis = jnp.concatenate([low[other], high[other]])
    prior = kernel(carry_kernel, start, [SMEM, VMEM, VMEM], depth, (), "carry", 2)(shift, own, prior_ends)
    partial = kernel(adjoint_chip_kernel, start, [VMEM] * 2, 6, (4, 2), "adjoint_chip", pad=PAD)(mismatch, chip_mis)
    slopes = kernel(slopes_kernel, start, [VMEM] * 3, depth, (), "slopes", fields=9)(own, chip, cross)
    sems = pltpu.SemaphoreType.DMA((4, depth))
    updated = kernel(adjoint_cross_kernel, start, [SMEM] + [VMEM] * 8, depth, (4, 4, 4, depth, depth), "adjoint_cross", out=HBM, extra=[sems])(
        step_size, own, chip, cross, mismatch, cross_mis, prior, slopes, partial
    )
    shown = kernel(copy_kernel, start, [VMEM], depth, name="publish")(mismatch)
    return updated[None], shown[None]


def solution(mesh):
    placed = P("tm", None, "gz", None, None)
    return jax.shard_map(
        per_device,
        mesh=mesh,
        in_specs=(placed, P(), P()),
        out_specs=(placed, placed),
        check_vma=False,
    )
```
